512 devices in a mesh: section: 8 (over x, z_hi), dp: 64 (over y, z_lo, core).
Axes of the slice: x: 4, y: 8, z: 8 (z_hi: 2, z_lo: 4; z = z_hi * 4 + z_lo), core: 2. Of those that a mesh axis runs over, the one named last changes fastest.
Arguments:
- activations: bfloat16 [8, 32, 512], P('section'), may hold values from -6 to 6
- out_grads: bfloat16 [8, 512, 53248], P('section', None, 'dp'), may hold values from -16 to 16
- master: float32 [8, 32, 53248], P('section', None, 'dp'), may hold values from -3 to 3
- moment_one: float32 [8, 32, 53248], P('section', None, 'dp'), may hold values from -3 to 3
- moment_two: float32 [8, 32, 53248], P('section', None, 'dp'), may hold values from 0.25 to 4
Outputs:
- to_previous: bfloat16 [8, 512, 32], P('section', 'dp')
- new_master: float32 [8, 32, 53248], P('section', None, 'dp')
- new_moment_one: float32 [8, 32, 53248], P('section', None, 'dp')
- new_moment_two: float32 [8, 32, 53248], P('section', None, 'dp')
- new_weights: bfloat16 [8, 32, 53248], P('section')
The draws below stay inside these ranges and needn't reach their ends.
All inputs are finite; a program needn't handle non-finite values.
Results may differ from the reference program's by a relative error of at most 0.0049.
Values may be sent and summed in bfloat16 or wider, within the bound.
A program may use at most 128 MiB of HBM per device.

```python
import math
import jax
import jax.numpy as jnp
from jax import lax

FF = 53248
SLAB = 32
TOKENS = 512
SECTIONS = 8
N_SECTION = 8


def strengthened(array, own_key, source, target, shards_of, factor):
    def block_of(dim):
        return (jnp.arange(array.shape[dim]) // (array.shape[dim] // shards_of)).reshape((-1,) + (1,) * (array.ndim - 1 - dim))

    near = jax.random.permutation(own_key, shards_of)[block_of(target)]
    far = (block_of(target) + shards_of // 2) % shards_of
    return jnp.where((block_of(source) == near) | (block_of(source) == far), factor * array, array)


def block_scale(stream_key, extent, shards, smallest, high):
    def one(dim, parts):
        steps = jax.random.uniform(jax.random.fold_in(jax.random.fold_in(stream_key, 6), dim), (parts,), jnp.float32, smallest / len(shards), high / len(shards))
        return jnp.repeat(jnp.exp(steps), extent[dim] // parts).reshape((-1,) + (1,) * (len(extent) - dim - 1))

    level = one(*shards[0])
    for cut in shards[1:]:
        level = level * one(*cut)
    return level


def centred(own_key, extent, deviation, limit, shards=(), held_as=jnp.bfloat16):
    array = deviation * jax.random.normal(own_key, extent, jnp.float32)
    if shards:
        array = array * block_scale(own_key, extent, shards, -0.22, 0.18)
    return jnp.clip(array, -limit, limit).astype(held_as)


def heavy_noise(stream_key, dims, deviation, most, shards, heavy, held_as=jnp.bfloat16):
    array = deviation * jax.random.normal(stream_key, dims, jnp.float32)
    if shards:
        array = array * block_scale(stream_key, dims, shards, -0.22, 0.18)
    return jnp.clip(strengthened(array, jax.random.fold_in(stream_key, 3), *heavy), -most, most).astype(held_as)


def setup_inputs(seed: int = 0) -> dict:
    keys = jax.random.split(jax.random.key(seed), 6)
    activations = centred(keys[0], (SECTIONS, SLAB, TOKENS), 1.0, 6.0, ((0, 8),))
    out_grads = heavy_noise(keys[1], (SECTIONS, TOKENS, FF), 1.0, 16.0, ((0, 8), (2, 64)), (2, 1, 64, 4.0))
    master = centred(keys[2], (SECTIONS, SLAB, FF), 0.5, 3.0, ((0, 8), (2, 64)), jnp.float32)
    moment_one = centred(keys[3], (SECTIONS, SLAB, FF), 0.5, 3.0, ((0, 8), (2, 64)), jnp.float32)
    moment_two = jnp.clip(jnp.exp(math.log(4.0) - 2.7725887 * jax.random.uniform(keys[4], (SECTIONS, SLAB, FF), jnp.float32) ** block_scale(keys[4], (SECTIONS, SLAB, FF), ((0, 8), (2, 64)), -0.2, 0.2)), 0.25, 4.0)
    return dict(activations=activations, out_grads=out_grads, master=master, moment_one=moment_one, moment_two=moment_two)


def reference(activations, out_grads, master, moment_one, moment_two):
    weights = master.astype(jnp.bfloat16)
    inputs = []
    grads = []
    for section in range(N_SECTION):
        inputs.append(lax.dot_general(out_grads[section], weights[section], (((1,), (1,)), ((), ())), preferred_element_type=jnp.float32).astype(jnp.bfloat16))
        grads.append(jnp.dot(activations[section], out_grads[section], preferred_element_type=jnp.float32))
    input_grad = jnp.stack(inputs)
    to_previous = jnp.concatenate([input_grad[1:], jnp.zeros_like(input_grad[:1])], axis=0)
    grad = jnp.stack(grads)
    total = jnp.sum(grad * grad)
    clip = jnp.minimum(1.0, math.sqrt(N_SECTION * FF * SLAB) / jnp.sqrt(total + 1e-06))
    scaled = clip * grad
    new_one = 0.9 * moment_one + 0.1 * scaled
    new_two = 0.95 * moment_two + 0.05 * scaled * scaled
    new_master = master - 0.05 * (new_one / (1.0 - 0.9 ** 10)) / (jnp.sqrt(new_two / (1.0 - 0.95 ** 10)) + 1e-08)
    return (to_previous, new_master, new_one, new_two, new_master.astype(jnp.bfloat16))
```

```python
import functools
import math

import jax
import jax.numpy as jnp
from jax import lax
from jax.experimental import pallas as pl
from jax.experimental.pallas import tpu as pltpu
from jax.sharding import PartitionSpec as P

FF = 53248
SLAB = 32
MESH = pl.DeviceIdType.MESH

NX, NY, NZ, NZL = 4, 8, 8, 4
COLS = FF // 64
WIDE = 2 * COLS
HALF = SLAB // 2
CUT = 9 * 128
SPLIT_STEPS = 5
VMEM_GRANT = 63250000


def adam(master, grad, one, two, clip):
    scaled = clip * grad
    new_one = 0.9 * one + 0.1 * scaled
    new_two = 0.95 * two + 0.05 * scaled * scaled
    new_master = master - 0.05 * (new_one / (1.0 - 0.9**10)) / (
        jnp.sqrt(new_two / (1.0 - 0.95**10)) + 1e-08
    )
    return new_master, new_one, new_two


def main_kernel(
    acts_hbm, og_hbm, master_hbm, one_hbm, two_hbm,
    w_out, master_out, one_out, two_out, prev_out,
    acts, og, state, other, norms, parts_a, got_a, part_b, got_b,
    load_sem, norm_send, norm_recv, pair_send, pair_recv,
    a_send, a_recv, b_send, b_recv,
    ring_full_send, ring_cut_send, ring_recv,
    core_send, core_recv, z_full_send, z_cut_send, z_full_recv, z_cut_recv,
):
    s = lax.axis_index("section")
    d = lax.axis_index("dp")
    x, zh = s // 2, s % 2
    y, zl, c = d // 8, (d // 2) % 4, d % 2
    z = zh * NZL + zl

    def dev(x, y, z, c):
        return {"section": x * 2 + z // NZL, "dp": (y * NZL + z % NZL) * 2 + c}

    mate = dev(x, y, z, 1 - c)

    places = (x * 2 + c, y, z)
    members = (
        lambda m: dev(m // 2, y, z, m % 2),
        lambda m: dev(x, m, z, c),
        lambda m: dev(x, y, m, c),
    )
    place_a = zl * 2 + c
    member_a = lambda m: dev(x, y, zh * NZL + m // 2, m % 2)

    barrier = pltpu.get_barrier_semaphore()

    def greet(members, place):
        def one(r, _):
            pl.semaphore_signal(
                barrier, inc=1, device_id=members((place + r) % 8), device_id_type=MESH
            )
            return 0

        lax.fori_loop(1, 8, one, 0)

    loads = [
        pltpu.make_async_copy(og_hbm, og, load_sem.at[0]),
        pltpu.make_async_copy(acts_hbm, acts, load_sem.at[1]),
        pltpu.make_async_copy(master_hbm, state.at[0], load_sem.at[2]),
        pltpu.make_async_copy(one_hbm, state.at[1], load_sem.at[3]),
        pltpu.make_async_copy(two_hbm, state.at[2], load_sem.at[4]),
    ]
    for load in loads:
        load.start()
    for p in range(3):
        greet(members[p], places[p])
    greet(member_a, place_a)

    loads[1].wait()
    loads[0].wait()
    grad = lax.dot_general(
        acts[...], og[...], (((1,), (1,)), ((), ())), preferred_element_type=jnp.float32
    )
    state[3] = grad
    norms[0, places[0]] = jnp.broadcast_to(jnp.sum(grad * grad), (1, 128))
    pl.semaphore_wait(barrier, 28)

    def norm_start(p):
        def one(r, _):
            pltpu.make_async_remote_copy(
                src_ref=norms.at[p, places[p]],
                dst_ref=norms.at[p, places[p]],
                send_sem=norm_send.at[p],
                recv_sem=norm_recv.at[p],
                device_id=members[p]((places[p] + r) % 8),
                device_id_type=MESH,
            ).start()
            return 0

        lax.fori_loop(1, 8, one, 0)

    def drain(ref, sem):
        pltpu.make_async_copy(ref, ref, sem).wait()

    def norm_finish(p):
        drain(norms.at[p, pl.ds(0, 7)], norm_recv.at[p])
        return jnp.sum(norms[p], axis=0)

    norm_start(0)

    for load in loads[2:]:
        load.wait()
    theirs = pl.ds(pl.multiple_of((1 - c) * HALF, HALF), HALF)
    mine = pl.ds(pl.multiple_of(c * HALF, HALF), HALF)
    for i in range(4):
        pltpu.make_async_remote_copy(
            src_ref=state.at[i, theirs],
            dst_ref=other.at[i],
            send_sem=pair_send.at[i],
            recv_sem=pair_recv.at[i],
            device_id=mate,
            device_id_type=MESH,
        ).start()

    weights = state[0].astype(jnp.bfloat16)
    partial = jnp.dot(weights, og[...], preferred_element_type=jnp.float32)
    turned = partial.T
    for j in range(8):
        for q in range(2):
            rows = [(4 * q + i) * 64 + j * 8 for i in range(4)]
            parts_a[j, q] = jnp.concatenate([turned[r : r + 8] for r in rows], axis=1)
    got_a[place_a] = parts_a[place_a]

    total = norm_finish(0)
    norms[1, places[1]] = total
    norm_start(1)

    def a_start(r, _):
        m = (place_a + r) % 8
        pltpu.make_async_remote_copy(
            src_ref=parts_a.at[m],
            dst_ref=got_a.at[place_a],
            send_sem=a_send,
            recv_sem=a_recv,
            device_id=member_a(m),
            device_id_type=MESH,
        ).start()
        return 0

    lax.fori_loop(1, 8, a_start, 0)

    total = norm_finish(1)
    norms[2, places[2]] = total
    norm_start(2)

    drain(got_a.at[pl.ds(0, 7)], a_recv)
    part_b[...] = jnp.sum(got_a[...], axis=0)
    for i in range(4):
        drain(other.at[i], pair_recv.at[i])

    total = norm_finish(2)
    limit = math.sqrt(8 * FF * SLAB)
    clip = jnp.minimum(1.0, limit / jnp.sqrt(total + 1e-06))[:, :1]

    own_w, _, _ = adam(state[0, mine], state[3, mine], state[1, mine], state[2, mine], clip)
    mate_w, _, _ = adam(other[0], other[3], other[1], other[2], clip)
    first = jnp.where(c == 0, own_w, mate_w)
    second = jnp.where(c == 0, mate_w, own_w)
    block = y * NZL + zl
    w_out[block, c] = jnp.concatenate([first, second], axis=1).astype(jnp.bfloat16)

    step = 1 - 2 * c
    ring_to = dev(x, (y + step + NY) % NY, z, c)

    def full(b):
        return w_out.at[b, c]

    def low(b):
        return w_out.at[b, c, :, pl.ds(0, CUT)]

    def high(b):
        return w_out.at[b, c, :, pl.ds(CUT, WIDE - CUT)]

    def send(ref, to, send_sem, recv_sem):
        pltpu.make_async_remote_copy(
            src_ref=ref, dst_ref=ref, send_sem=send_sem, recv_sem=recv_sem,
            device_id=to, device_id_type=MESH,
        ).start()

    def z_other(j):
        return (zl + j) % NZL

    def z_dev(j):
        return dev(x, y, zh * NZL + z_other(j), c)

    send(full(block), ring_to, ring_full_send, ring_recv.at[block])
    for j in (1, 3, 2):
        send(full(block), z_dev(j), z_full_send, z_full_recv.at[zl])
    send(full(block), mate, core_send, core_recv)

    new_master, new_one, new_two = adam(state[0], state[3], state[1], state[2], clip)
    master_out[...] = new_master
    one_out[...] = new_one
    two_out[...] = new_two

    @pl.when(s > 0)
    def _():
        def b_start(m, _):
            pltpu.make_async_remote_copy(
                src_ref=part_b.at[m // 4],
                dst_ref=got_b.at[y],
                send_sem=b_send,
                recv_sem=b_recv,
                device_id={"section": s - 1, "dp": (m * NZL + zl) * 2 + c},
                device_id_type=MESH,
            ).start()
            return 0

        lax.fori_loop(0, NY, b_start, 0)

    def source(k):
        return ((y - step * k + 2 * NY) % NY) * NZL

    def z_home(j):
        b = y * NZL + z_other(j)
        drain(full(b), z_full_recv.at[z_other(j)])
        send(low(b), ring_to, ring_cut_send, ring_recv.at[b])
        send(full(b), mate, core_send, core_recv)

    def ring_own(k, cut_now, last):
        b = source(k) + zl
        drain(full(b), ring_recv.at[b])
        if not last:
            send(full(b), ring_to, ring_full_send, ring_recv.at[b])
        if cut_now:
            for j in (1, 3, 2):
                send(high(b), z_dev(j), z_cut_send, z_cut_recv.at[b])
        send(full(b), mate, core_send, core_recv)

    def ring_other(k, j, cut_now, cut_next, last):
        b = source(k) + z_other(j)
        ref = low(b) if cut_now else full(b)
        drain(ref, ring_recv.at[b])
        if not last:
            if cut_next:
                send(low(b), ring_to, ring_cut_send, ring_recv.at[b])
            else:
                send(full(b), ring_to, ring_full_send, ring_recv.at[b])
        send(ref, mate, core_send, core_recv)

    def z_high(k):
        for j in (1, 3, 2):
            b = source(k) + z_other(j)
            drain(high(b), z_cut_recv.at[b])
            send(high(b), mate, core_send, core_recv)

    ring_own(1, True, False)
    for j in (1, 3, 2):
        z_home(j)
    for k in range(1, NY):
        if k > 1:
            ring_own(k, k <= SPLIT_STEPS, k == NY - 1)
        if k == SPLIT_STEPS:
            z_high(k - 2)
            z_high(k - 1)
            z_high(k)
        elif 3 <= k < SPLIT_STEPS:
            z_high(k - 2)
        for j in (1, 3, 2):
            ring_other(k, j, k <= SPLIT_STEPS, k + 1 <= SPLIT_STEPS, k == NY - 1)

    @pl.when(s < 7)
    def _():
        drain(got_b, b_recv)
        tile = jnp.sum(got_b[...], axis=0)
        tile = pltpu.roll(tile, (128 - (y % 4) * SLAB) % 128, 1)
        prev_out[...] = tile[:, :SLAB].astype(jnp.bfloat16)

    @pl.when(s == 7)
    def _():
        prev_out[...] = jnp.zeros_like(prev_out)

    for p in range(3):
        drain(norms.at[p, pl.ds(0, 7)], norm_send.at[p])
    for i in range(4):
        drain(other.at[i], pair_send.at[i])
    drain(got_a.at[pl.ds(0, 7)], a_send)

    @pl.when(s > 0)
    def _():
        drain(got_b, b_send)

    n_cut = 3 * SPLIT_STEPS
    n_full = 4 * (NY - 1) - n_cut
    drain(w_out.at[pl.ds(0, n_full), c], ring_full_send)
    drain(w_out.at[pl.ds(0, n_cut), c, :, pl.ds(0, CUT)], ring_cut_send)
    drain(w_out.at[pl.ds(0, 3), c], z_full_send)
    drain(w_out.at[pl.ds(0, n_cut), c, :, pl.ds(CUT, WIDE - CUT)], z_cut_send)
    drain(w_out.at[:, 1 - c], core_recv)
    drain(w_out.at[:, c], core_send)


def write_kernel(
    w, master, one, two, prev, prev_hbm, master_hbm, one_hbm, two_hbm, w_hbm, sem
):
    copies = []
    for b in range(32):
        for h in range(2):
            copies.append(
                pltpu.make_async_copy(
                    w.at[b, h],
                    w_hbm.at[0, pl.ds(h * HALF, HALF), pl.ds(b * WIDE, WIDE)],
                    sem.at[b],
                )
            )
    small = [
        pltpu.make_async_copy(prev, prev_hbm.at[0], sem.at[32]),
        pltpu.make_async_copy(master, master_hbm.at[0], sem.at[33]),
        pltpu.make_async_copy(one, one_hbm.at[0], sem.at[34]),
        pltpu.make_async_copy(two, two_hbm.at[0], sem.at[35]),
    ]
    for copy in small + copies:
        copy.start()
    for copy in small + copies:
        copy.wait()


def body(activations, out_grads, master, moment_one, moment_two):
    f32, bf16 = jnp.float32, jnp.bfloat16
    hbm = pl.BlockSpec(memory_space=pltpu.HBM)
    vmem = pl.BlockSpec(memory_space=pltpu.VMEM)
    dma = pltpu.SemaphoreType.DMA
    kept = pl.pallas_call(
        main_kernel,
        out_shape=(
            pltpu.VMEM((32, 2, HALF, WIDE), bf16),
            pltpu.VMEM((SLAB, COLS), f32),
            pltpu.VMEM((SLAB, COLS), f32),
            pltpu.VMEM((SLAB, COLS), f32),
            pltpu.VMEM((8, SLAB), bf16),
        ),
        in_specs=[hbm] * 5,
        out_specs=[vmem] * 5,
        scratch_shapes=[
            pltpu.VMEM((SLAB, 512), bf16),
            pltpu.VMEM((COLS, 512), bf16),
            pltpu.VMEM((4, SLAB, COLS), f32),
            pltpu.VMEM((4, HALF, COLS), f32),
            pltpu.VMEM((3, 8, 1, 128), f32),
            pltpu.VMEM((8, 2, 8, 128), f32),
            pltpu.VMEM((8, 2, 8, 128), f32),
            pltpu.VMEM((2, 8, 128), f32),
            pltpu.VMEM((8, 8, 128), f32),
            dma((5,)), dma((3,)), dma((3,)), dma((4,)), dma((4,)),
            dma, dma, dma, dma,
            dma, dma, dma((32,)),
            dma, dma, dma, dma, dma((4,)), dma((32,)),
        ],
        compiler_params=pltpu.CompilerParams(
            collective_id=0, has_side_effects=True, vmem_limit_bytes=VMEM_GRANT
        ),
        name="update_and_gather",
    )(
        activations[0],
        jnp.swapaxes(out_grads, 1, 2)[0],
        master[0],
        moment_one[0],
        moment_two[0],
    )
    shapes = (
        jax.ShapeDtypeStruct((1, 8, SLAB), bf16),
        jax.ShapeDtypeStruct((1, SLAB, COLS), f32),
        jax.ShapeDtypeStruct((1, SLAB, COLS), f32),
        jax.ShapeDtypeStruct((1, SLAB, COLS), f32),
        jax.ShapeDtypeStruct((1, SLAB, FF), bf16),
    )
    return pl.pallas_call(
        write_kernel,
        out_shape=shapes,
        in_specs=[vmem] * 5,
        out_specs=[hbm] * 5,
        scratch_shapes=[dma((36,))],
        compiler_params=pltpu.CompilerParams(vmem_limit_bytes=8 << 20),
        name="write_out",
    )(*kept)


def solution(mesh):
    placed = (
        P("section", None, None),
        P("section", None, "dp"),
        P("section", None, "dp"),
        P("section", None, "dp"),
        P("section", None, "dp"),
    )
    return jax.shard_map(
        body,
        mesh=mesh,
        in_specs=placed,
        out_specs=(
            P("section", "dp", None),
            P("section", None, "dp"),
            P("section", None, "dp"),
            P("section", None, "dp"),
            P("section", None, None),
        ),
        check_vma=False,
    )
```

```python
import functools
import math

import jax
import jax.numpy as jnp
from jax import lax
from jax.experimental import pallas as pl
from jax.experimental.pallas import tpu as pltpu
from jax.sharding import PartitionSpec as P

FF = 53248
SLAB = 32
MESH = pl.DeviceIdType.MESH

NX, NY, NZ, NZL = 4, 8, 8, 4
COLS = FF // 64
WIDE = 2 * COLS
HALF = SLAB // 2
def hops(by, size):
    return min(by, size - by)


NEAR_STEPS = sorted(
    ((dz, dc) for dz in range(NZ) for dc in range(2) if dz or dc), key=lambda m: -hops(m[0], NZ)
)
FLAT_STEPS = sorted(
    ((dx, dy) for dx in range(NX) for dy in range(NY) if dx or dy),
    key=lambda m: -hops(m[0], NX) - hops(m[1], NY),
)
REACH = {1: 4, -1: 3}
OWN_HOPS = ((3, 4), (2, 3), (1, 2), (0, 1))
OTHER_HOPS = ((2, 4), (2, 3), (1, 2), (0, 1))
CUTS = (11, 11, 9, 9, 9)
TILES = WIDE // 128
ORDER = (
    ("own", 1, 1, 0), ("own", -1, 1, 0), ("home", 1, 0, 3), ("home", 1, 0, 1), ("high", 1, 0, 3),
    ("high", 1, 0, 1), ("own", 1, 2, 0), ("high", 1, 1, 3), ("own", -1, 2, 0), ("home", 1, 0, 2),
    ("high", 1, 1, 1), ("high", 1, 0, 2), ("high", -1, 1, 3), ("high", -1, 1, 1), ("high", 1, 1, 2),
    ("low", 1, 1, 3), ("low", -1, 1, 3), ("high", -1, 1, 2), ("low", 1, 1, 1), ("low", -1, 1, 1),
    ("high", 1, 2, 3), ("high", 1, 2, 1), ("own", 1, 3, 0), ("high", -1, 2, 3), ("low", 1, 1, 2),
    ("high", 1, 2, 2), ("high", -1, 2, 1), ("low", -1, 1, 2), ("own", -1, 3, 0), ("low", 1, 2, 3),
    ("high", -1, 2, 2), ("low", -1, 2, 3), ("low", 1, 2, 1), ("low", -1, 2, 1), ("low", 1, 2, 2),
    ("low", -1, 2, 2), ("high", 1, 3, 3), ("high", 1, 3, 1), ("own", 1, 4, 0), ("high", 1, 3, 2),
    ("high", -1, 3, 3), ("low", -1, 3, 3), ("high", -1, 3, 1), ("high", -1, 3, 2), ("low", 1, 3, 3),
    ("low", -1, 3, 1), ("low", 1, 4, 3), ("low", -1, 3, 2), ("low", 1, 3, 1), ("low", 1, 4, 1),
    ("low", 1, 3, 2), ("low", 1, 4, 2), ("high", 1, 4, 3), ("high", 1, 4, 1), ("high", 1, 4, 2),
)
VMEM_GRANT = 63250000


def adam(master, grad, one, two, clip):
    scaled = clip * grad
    new_one = 0.9 * one + 0.1 * scaled
    new_two = 0.95 * two + 0.05 * scaled * scaled
    new_master = master - 0.05 * (new_one / (1.0 - 0.9**10)) / (
        jnp.sqrt(new_two / (1.0 - 0.95**10)) + 1e-08
    )
    return new_master, new_one, new_two


def main_kernel(
    acts_hbm, og_hbm, master_hbm, one_hbm, two_hbm,
    w_out, master_out, one_out, two_out, prev_out,
    acts, og, state, other, norms_near, norms_flat, turned, parts_a, got_a, part_b, got_b,
    load_sem, norm_send, norm_recv, pair_send, pair_recv,
    a_send, a_recv, b_send, b_recv,
    gather_send, ring_recv, core_send, core_recv, z_full_recv, z_cut_recv,
):
    s = lax.axis_index("section")
    d = lax.axis_index("dp")
    div, rem = lax.div, lax.rem
    norms = (norms_near, norms_flat)
    x, zh = div(s, 2), rem(s, 2)
    y, zl, c = div(d, 8), rem(div(d, 2), NZL), rem(d, 2)
    z = zh * NZL + zl

    def dev(x, y, z, c):
        return {"section": x * 2 + div(z, NZL), "dp": (y * NZL + rem(z, NZL)) * 2 + c}

    mate = dev(x, y, z, 1 - c)

    def ring8(a, by):
        return rem(a + by, 8)

    near = [dev(x, y, ring8(z, dz), rem(c + dc, 2)) for dz, dc in NEAR_STEPS]
    flat = [dev(rem(x + dx, NX), ring8(y, dy), z, c) for dx, dy in FLAT_STEPS]
    groups = (near, flat)
    places = (z * 2 + c, x * NY + y)
    place_a = zl * 2 + c
    group_a = [
        (rem(zl + dz, NZL) * 2 + rem(c + dc, 2), rem(zl + dz, NZL), rem(c + dc, 2))
        for dz in range(NZL)
        for dc in range(2)
        if dz or dc
    ]

    barrier = pltpu.get_barrier_semaphore()

    def greet(who):
        pl.semaphore_signal(barrier, inc=1, device_id=who, device_id_type=MESH)

    loads = [
        pltpu.make_async_copy(og_hbm, og, load_sem.at[0]),
        pltpu.make_async_copy(acts_hbm, acts, load_sem.at[1]),
        pltpu.make_async_copy(master_hbm, state.at[0], load_sem.at[2]),
        pltpu.make_async_copy(one_hbm, state.at[1], load_sem.at[3]),
        pltpu.make_async_copy(two_hbm, state.at[2], load_sem.at[4]),
    ]
    for load in loads:
        load.start()
    for group in groups:
        for who in group:
            greet(who)

    loads[1].wait()
    loads[0].wait()
    grad = lax.dot_general(
        acts[...], og[...], (((1,), (1,)), ((), ())), preferred_element_type=jnp.float32
    )
    state[3] = grad
    norms[0][places[0]] = jnp.broadcast_to(jnp.sum(grad * grad), (1, 128))
    pl.semaphore_wait(barrier, len(groups[0]) + len(groups[1]))

    def norm_start(p):
        for who in groups[p]:
            pltpu.make_async_remote_copy(
                src_ref=norms[p].at[places[p]],
                dst_ref=norms[p].at[places[p]],
                send_sem=norm_send.at[p],
                recv_sem=norm_recv.at[p],
                device_id=who,
                device_id_type=MESH,
            ).start()

    def drain(ref, sem):
        pltpu.make_async_copy(ref, ref, sem).wait()

    def norm_finish(p):
        drain(norms[p].at[pl.ds(0, len(groups[p]))], norm_recv.at[p])
        return jnp.sum(norms[p][...], axis=0)

    norm_start(0)

    for load in loads[2:]:
        load.wait()
    theirs = pl.ds(pl.multiple_of((1 - c) * HALF, HALF), HALF)
    mine = pl.ds(pl.multiple_of(c * HALF, HALF), HALF)
    for i in range(4):
        pltpu.make_async_remote_copy(
            src_ref=state.at[i, theirs],
            dst_ref=other.at[i],
            send_sem=pair_send.at[i],
            recv_sem=pair_recv.at[i],
            device_id=mate,
            device_id_type=MESH,
        ).start()

    weights = state[0].astype(jnp.bfloat16)
    partial = jnp.dot(weights, og[...], preferred_element_type=jnp.float32)
    turned[...] = partial.T
    for j in range(8):
        for u in range(2):
            rows = [pl.ds(j * 8 + u * 4 + i, NY, stride=64) for i in range(4)]
            parts_a[j, u] = jnp.concatenate([turned[r] for r in rows], axis=1)
    got_a[place_a] = parts_a[place_a]
    for m, to_zl, to_c in group_a:
        pltpu.make_async_remote_copy(
            src_ref=parts_a.at[m],
            dst_ref=got_a.at[place_a],
            send_sem=a_send,
            recv_sem=a_recv,
            device_id=dev(x, y, zh * NZL + to_zl, to_c),
            device_id_type=MESH,
        ).start()

    total = norm_finish(0)
    norms[1][places[1]] = total
    norm_start(1)

    drain(got_a.at[pl.ds(0, 7)], a_recv)
    for u in range(2):
        rows = jnp.sum(got_a[:, u], axis=0)
        for m in range(NY):
            part_b[m, u] = rows[m]

    for i in range(4):
        drain(other.at[i], pair_recv.at[i])

    total = norm_finish(1)
    limit = math.sqrt(8 * FF * SLAB)
    clip = jnp.minimum(1.0, limit / jnp.sqrt(total + 1e-06))[:, :1]

    own_w, _, _ = adam(state[0, mine], state[3, mine], state[1, mine], state[2, mine], clip)
    mate_w, _, _ = adam(other[0], other[3], other[1], other[2], clip)
    first = jnp.where(c == 0, own_w, mate_w)
    second = jnp.where(c == 0, mate_w, own_w)
    block = y * NZL + zl
    whole = jnp.concatenate([first, second], axis=1).astype(jnp.bfloat16)
    w_out[c, block] = whole

    ahead = 1 - 2 * c

    def ring_to(side, hops):
        return dev(x, rem(y + ahead * side * hops + NY, NY), z, c)

    def tiles(b, start, stop):
        return w_out.at[c, b, :, pl.ds(start * 128, (stop - start) * 128)]

    sent = {}

    def send(b, start, stop, to, recv_sem):
        size = stop - start
        sent[size] = sent.get(size, 0) + 1
        ref = tiles(b, start, stop)
        pltpu.make_async_remote_copy(
            src_ref=ref, dst_ref=ref, send_sem=gather_send.at[size], recv_sem=recv_sem,
            device_id=to, device_id_type=MESH,
        ).start()

    def to_mate(b, start, stop):
        ref = tiles(b, start, stop)
        pltpu.make_async_remote_copy(
            src_ref=ref, dst_ref=ref, send_sem=core_send, recv_sem=core_recv,
            device_id=mate, device_id_type=MESH,
        ).start()

    def z_other(j):
        return rem(zl + j, NZL)

    def z_dev(j):
        return dev(x, y, zh * NZL + z_other(j), c)

    def own_on(b, side, k):
        for start, stop in OWN_HOPS:
            if start == k and stop <= REACH[side]:
                send(b, 0, TILES, ring_to(side, stop - start), ring_recv.at[b])

    def other_on(b, side, k):
        for start, stop in OTHER_HOPS:
            if start == k and stop <= REACH[side] and CUTS[stop]:
                send(b, 0, CUTS[stop], ring_to(side, stop - start), ring_recv.at[b])

    def high_on(b, k):
        if CUTS[k] < TILES:
            for j in (1, 3, 2):
                send(b, CUTS[k], TILES, z_dev(j), z_cut_recv.at[b])

    for side in REACH:
        own_on(block, side, 0)
    for j in (1, 3, 2):
        send(block, 0, CUTS[0], z_dev(j), z_full_recv.at[zl])
    high_on(block, 0)
    to_mate(block, 0, TILES)

    @pl.when(s > 0)
    def _():
        for m in range(NY):
            pltpu.make_async_remote_copy(
                src_ref=part_b.at[m],
                dst_ref=got_b.at[y],
                send_sem=b_send,
                recv_sem=b_recv,
                device_id={"section": s - 1, "dp": (m * NZL + zl) * 2 + c},
                device_id_type=MESH,
            ).start()

    new_master, new_one, new_two = adam(state[0], state[3], state[1], state[2], clip)
    master_out[...] = new_master
    one_out[...] = new_one
    two_out[...] = new_two

    def source(side, k):
        return rem(y - ahead * side * k + NY, NY) * NZL

    for what, side, k, j in ORDER:
        b = source(side, k) + z_other(j)
        if what == "own":
            drain(tiles(b, 0, TILES), ring_recv.at[b])
            own_on(b, side, k)
            high_on(b, k)
            to_mate(b, 0, TILES)
        elif what == "home":
            drain(tiles(b, 0, CUTS[0]), z_full_recv.at[z_other(j)])
            for out in REACH:
                other_on(b, out, 0)
            to_mate(b, 0, CUTS[0])
        elif what == "low":
            drain(tiles(b, 0, CUTS[k]), ring_recv.at[b])
            other_on(b, side, k)
            to_mate(b, 0, CUTS[k])
        else:
            drain(tiles(b, CUTS[k], TILES), z_cut_recv.at[b])
            to_mate(b, CUTS[k], TILES)

    @pl.when(s < 7)
    def _():
        drain(got_b, b_recv)
        rows = jnp.sum(got_b[...], axis=0)
        rows = [rows[u : u + 1, i * SLAB : (i + 1) * SLAB] for u in range(2) for i in range(4)]
        prev_out[...] = jnp.concatenate(rows, axis=0).astype(jnp.bfloat16)

    @pl.when(s == 7)
    def _():
        prev_out[...] = jnp.zeros_like(prev_out)

    for p, group in enumerate(groups):
        drain(norms[p].at[pl.ds(0, len(group))], norm_send.at[p])
    for i in range(4):
        drain(other.at[i], pair_send.at[i])
    drain(got_a.at[pl.ds(0, 7)], a_send)

    @pl.when(s > 0)
    def _():
        drain(got_b, b_send)

    for size, count in sorted(sent.items()):
        drain(w_out.at[0, pl.ds(0, count), :, pl.ds(0, size * 128)], gather_send.at[size])
    drain(w_out.at[1 - c], core_recv)
    drain(w_out.at[c], core_send)


def write_kernel(
    w, master, one, two, prev, prev_hbm, master_hbm, one_hbm, two_hbm, w_hbm, sem
):
    copies = []
    for h in range(2):
        rows = pl.ds(h * HALF, HALF)
        for b in range(32):
            copies.append(
                pltpu.make_async_copy(w.at[h, b], w_hbm.at[0, rows, pl.ds(b * WIDE, WIDE)], sem.at[b])
            )
    small = [
        pltpu.make_async_copy(prev, prev_hbm.at[0], sem.at[32 + 0]),
        pltpu.make_async_copy(master, master_hbm.at[0], sem.at[32 + 1]),
        pltpu.make_async_copy(one, one_hbm.at[0], sem.at[32 + 2]),
        pltpu.make_async_copy(two, two_hbm.at[0], sem.at[32 + 3]),
    ]
    for copy in small + copies:
        copy.start()
    for copy in small + copies:
        copy.wait()


def body(activations, out_grads, master, moment_one, moment_two):
    f32, bf16 = jnp.float32, jnp.bfloat16
    hbm = pl.BlockSpec(memory_space=pltpu.HBM)
    vmem = pl.BlockSpec(memory_space=pltpu.VMEM)
    dma = pltpu.SemaphoreType.DMA
    kept = pl.pallas_call(
        main_kernel,
        out_shape=(
            pltpu.VMEM((2, 32, HALF, WIDE), bf16),
            pltpu.VMEM((SLAB, COLS), f32),
            pltpu.VMEM((SLAB, COLS), f32),
            pltpu.VMEM((SLAB, COLS), f32),
            pltpu.VMEM((8, SLAB), bf16),
        ),
        in_specs=[hbm] * 5,
        out_specs=[vmem] * 5,
        scratch_shapes=[
            pltpu.VMEM((SLAB, 512), bf16),
            pltpu.VMEM((COLS, 512), bf16),
            pltpu.VMEM((4, SLAB, COLS), f32),
            pltpu.VMEM((4, HALF, COLS), f32),
            pltpu.VMEM((2 * NZ, 1, 128), f32),
            pltpu.VMEM((NX * NY, 1, 128), f32),
            pltpu.VMEM((512, SLAB), f32),
            pltpu.VMEM((8, 2, NY, 128), f32),
            pltpu.VMEM((8, 2, NY, 128), f32),
            pltpu.VMEM((NY, 2, 128), f32),
            pltpu.VMEM((NY, 2, 128), f32),
            dma((5,)), dma((2,)), dma((2,)), dma((4,)), dma((4,)),
            dma, dma, dma, dma,
            dma((TILES + 1,)), dma((32,)), dma, dma, dma((NZL,)), dma((32,)),
        ],
        compiler_params=pltpu.CompilerParams(
            collective_id=0, has_side_effects=True, vmem_limit_bytes=VMEM_GRANT
        ),
        name="update_and_gather",
    )(
        activations[0],
        jnp.swapaxes(out_grads, 1, 2)[0],
        master[0],
        moment_one[0],
        moment_two[0],
    )
    shapes = (
        jax.ShapeDtypeStruct((1, 8, SLAB), bf16),
        jax.ShapeDtypeStruct((1, SLAB, COLS), f32),
        jax.ShapeDtypeStruct((1, SLAB, COLS), f32),
        jax.ShapeDtypeStruct((1, SLAB, COLS), f32),
        jax.ShapeDtypeStruct((1, SLAB, FF), bf16),
    )
    return pl.pallas_call(
        write_kernel,
        out_shape=shapes,
        in_specs=[vmem] * 5,
        out_specs=[hbm] * 5,
        scratch_shapes=[dma((36,))],
        compiler_params=pltpu.CompilerParams(vmem_limit_bytes=8 << 20),
        name="write_out",
    )(*kept)


def solution(mesh):
    placed = (
        P("section", None, None),
        P("section", None, "dp"),
        P("section", None, "dp"),
        P("section", None, "dp"),
        P("section", None, "dp"),
    )
    return jax.shard_map(
        body,
        mesh=mesh,
        in_specs=placed,
        out_specs=(
            P("section", "dp", None),
            P("section", None, "dp"),
            P("section", None, "dp"),
            P("section", None, "dp"),
            P("section", None, None),
        ),
        check_vma=False,
    )
```

```python
import functools
import math

import jax
import jax.numpy as jnp
from jax import lax
from jax.experimental import pallas as pl
from jax.experimental.pallas import tpu as pltpu
from jax.sharding import PartitionSpec as P

FF = 53248
SLAB = 32
MESH = pl.DeviceIdType.MESH

NX, NY, NZ, NZL = 4, 8, 8, 4
COLS = FF // 64
WIDE = 2 * COLS
HALF = SLAB // 2
def hops(by, size):
    return min(by, size - by)


NEAR_STEPS = sorted(
    ((dz, dc) for dz in range(NZ) for dc in range(2) if dz or dc), key=lambda m: -hops(m[0], NZ)
)
FLAT_STEPS = sorted(
    ((dx, dy) for dx in range(NX) for dy in range(NY) if dx or dy),
    key=lambda m: -hops(m[0], NX) - hops(m[1], NY),
)
REACH = {1: 4, -1: 3}
OWN_HOPS = ((3, 4), (2, 3), (1, 2), (0, 1))
OTHER_HOPS = ((2, 4), (2, 3), (1, 2), (0, 1))
CUTS = (10, 10, 9, 9, 9)
TILES = WIDE // 128
HAND_OFF_TURN = 14
ORDER = (
    ("own", 1, 1, 0), ("own", -1, 1, 0), ("home", 1, 0, 3), ("home", 1, 0, 1), ("high", 1, 0, 3),
    ("high", 1, 0, 1), ("own", 1, 2, 0), ("home", 1, 0, 2), ("own", -1, 2, 0), ("high", 1, 1, 3),
    ("high", 1, 1, 1), ("high", 1, 0, 2), ("high", -1, 1, 3), ("low", 1, 1, 3), ("high", -1, 1, 1),
    ("low", -1, 1, 3), ("high", 1, 1, 2), ("low", 1, 1, 1), ("low", -1, 1, 1), ("high", -1, 1, 2),
    ("high", 1, 2, 3), ("high", 1, 2, 1), ("own", 1, 3, 0), ("low", -1, 1, 2), ("low", 1, 1, 2),
    ("high", -1, 2, 3), ("high", 1, 2, 2), ("high", -1, 2, 1), ("own", -1, 3, 0), ("low", 1, 2, 3),
    ("high", -1, 2, 2), ("low", -1, 2, 3), ("low", 1, 2, 1), ("low", -1, 2, 1), ("low", 1, 2, 2),
    ("low", -1, 2, 2), ("high", 1, 3, 3), ("high", 1, 3, 1), ("own", 1, 4, 0), ("high", 1, 3, 2),
    ("high", -1, 3, 3), ("high", -1, 3, 1), ("low", -1, 3, 3), ("high", -1, 3, 2), ("low", 1, 3, 3),
    ("low", -1, 3, 1), ("low", 1, 4, 3), ("low", -1, 3, 2), ("low", 1, 3, 1), ("low", 1, 4, 1),
    ("high", 1, 4, 3), ("low", 1, 3, 2), ("high", 1, 4, 1), ("low", 1, 4, 2), ("high", 1, 4, 2),
)
VMEM_GRANT = 63250000


def adam(master, grad, one, two, clip):
    scaled = clip * grad
    new_one = 0.9 * one + 0.1 * scaled
    new_two = 0.95 * two + 0.05 * scaled * scaled
    new_master = master - 0.05 * (new_one / (1.0 - 0.9**10)) / (
        jnp.sqrt(new_two / (1.0 - 0.95**10)) + 1e-08
    )
    return new_master, new_one, new_two


def main_kernel(
    acts_hbm, og_hbm, master_hbm, one_hbm, two_hbm,
    w_out, master_out, one_out, two_out, prev_out,
    acts, og, state, other, norms_near, norms_flat, turned, parts_a, got_a, part_b, got_b,
    load_sem, norm_send, norm_recv, pair_send, pair_recv,
    a_send, a_recv, b_send, b_recv,
    gather_send, ring_recv, core_send, core_recv, z_full_recv, z_cut_recv,
):
    s = lax.axis_index("section")
    d = lax.axis_index("dp")
    div, rem = lax.div, lax.rem
    norms = (norms_flat, norms_near)
    x, zh = div(s, 2), rem(s, 2)
    y, zl, c = div(d, 8), rem(div(d, 2), NZL), rem(d, 2)
    z = zh * NZL + zl

    def dev(x, y, z, c):
        return {"section": x * 2 + div(z, NZL), "dp": (y * NZL + rem(z, NZL)) * 2 + c}

    mate = dev(x, y, z, 1 - c)

    def ring8(a, by):
        return rem(a + by, 8)

    near = [dev(x, y, ring8(z, dz), rem(c + dc, 2)) for dz, dc in NEAR_STEPS]
    flat = [dev(rem(x + dx, NX), ring8(y, dy), z, c) for dx, dy in FLAT_STEPS]
    groups = (flat, near)
    places = (x * NY + y, z * 2 + c)
    place_a = zl * 2 + c
    group_a = [
        (rem(zl + dz, NZL) * 2 + rem(c + dc, 2), rem(zl + dz, NZL), rem(c + dc, 2))
        for dz in range(NZL)
        for dc in range(2)
        if dz or dc
    ]

    barrier = pltpu.get_barrier_semaphore()

    def greet(who):
        pl.semaphore_signal(barrier, inc=1, device_id=who, device_id_type=MESH)

    loads = [
        pltpu.make_async_copy(og_hbm, og, load_sem.at[0]),
        pltpu.make_async_copy(acts_hbm, acts, load_sem.at[1]),
        pltpu.make_async_copy(master_hbm, state.at[0], load_sem.at[2]),
        pltpu.make_async_copy(one_hbm, state.at[1], load_sem.at[3]),
        pltpu.make_async_copy(two_hbm, state.at[2], load_sem.at[4]),
    ]
    for load in loads:
        load.start()
    for group in groups:
        for who in group:
            greet(who)

    loads[1].wait()
    loads[0].wait()
    grad = lax.dot_general(
        acts[...], og[...], (((1,), (1,)), ((), ())), preferred_element_type=jnp.float32
    )
    state[3] = grad
    norms[0][places[0]] = jnp.broadcast_to(jnp.sum(grad * grad), (1, 128))
    pl.semaphore_wait(barrier, len(groups[0]) + len(groups[1]))

    def norm_start(p):
        for who in groups[p]:
            pltpu.make_async_remote_copy(
                src_ref=norms[p].at[places[p]],
                dst_ref=norms[p].at[places[p]],
                send_sem=norm_send.at[p],
                recv_sem=norm_recv.at[p],
                device_id=who,
                device_id_type=MESH,
            ).start()

    def drain(ref, sem):
        pltpu.make_async_copy(ref, ref, sem).wait()

    def norm_finish(p):
        drain(norms[p].at[pl.ds(0, len(groups[p]))], norm_recv.at[p])
        return jnp.sum(norms[p][...], axis=0)

    norm_start(0)

    for load in loads[2:]:
        load.wait()
    theirs = pl.ds(pl.multiple_of((1 - c) * HALF, HALF), HALF)
    mine = pl.ds(pl.multiple_of(c * HALF, HALF), HALF)
    for i in range(4):
        pltpu.make_async_remote_copy(
            src_ref=state.at[i, theirs],
            dst_ref=other.at[i],
            send_sem=pair_send.at[i],
            recv_sem=pair_recv.at[i],
            device_id=mate,
            device_id_type=MESH,
        ).start()

    weights = state[0].astype(jnp.bfloat16)
    partial = jnp.dot(weights, og[...], preferred_element_type=jnp.float32)
    turned[...] = partial.T
    for j in range(8):
        for u in range(2):
            rows = [pl.ds(j * 8 + u * 4 + i, NY, stride=64) for i in range(4)]
            parts_a[j, u] = jnp.concatenate([turned[r] for r in rows], axis=1)
    got_a[place_a] = parts_a[place_a]
    for m, to_zl, to_c in group_a:
        pltpu.make_async_remote_copy(
            src_ref=parts_a.at[m],
            dst_ref=got_a.at[place_a],
            send_sem=a_send,
            recv_sem=a_recv,
            device_id=dev(x, y, zh * NZL + to_zl, to_c),
            device_id_type=MESH,
        ).start()

    total = norm_finish(0)
    norms[1][places[1]] = total
    norm_start(1)

    drain(got_a.at[pl.ds(0, 7)], a_recv)
    for u in range(2):
        rows = jnp.sum(got_a[:, u], axis=0)
        for m in range(NY):
            part_b[m, u] = rows[m]

    for i in range(4):
        drain(other.at[i], pair_recv.at[i])

    total = norm_finish(1)
    limit = math.sqrt(8 * FF * SLAB)
    clip = jnp.minimum(1.0, limit / jnp.sqrt(total + 1e-06))[:, :1]

    own_w, _, _ = adam(state[0, mine], state[3, mine], state[1, mine], state[2, mine], clip)
    mate_w, _, _ = adam(other[0], other[3], other[1], other[2], clip)
    first = jnp.where(c == 0, own_w, mate_w)
    second = jnp.where(c == 0, mate_w, own_w)
    block = y * NZL + zl
    whole = jnp.concatenate([first, second], axis=1).astype(jnp.bfloat16)
    w_out[c, block] = whole

    ahead = 1 - 2 * c

    def ring_to(side, hops):
        return dev(x, rem(y + ahead * side * hops + NY, NY), z, c)

    def tiles(b, start, stop):
        return w_out.at[c, b, :, pl.ds(start * 128, (stop - start) * 128)]

    sent = {}

    def send(b, start, stop, to, recv_sem):
        size = stop - start
        sent[size] = sent.get(size, 0) + 1
        ref = tiles(b, start, stop)
        pltpu.make_async_remote_copy(
            src_ref=ref, dst_ref=ref, send_sem=gather_send.at[size], recv_sem=recv_sem,
            device_id=to, device_id_type=MESH,
        ).start()

    def to_mate(b, start, stop):
        ref = tiles(b, start, stop)
        pltpu.make_async_remote_copy(
            src_ref=ref, dst_ref=ref, send_sem=core_send, recv_sem=core_recv,
            device_id=mate, device_id_type=MESH,
        ).start()

    def z_other(j):
        return rem(zl + j, NZL)

    def z_dev(j):
        return dev(x, y, zh * NZL + z_other(j), c)

    def own_on(b, side, k):
        for start, stop in OWN_HOPS:
            if start == k and stop <= REACH[side]:
                send(b, 0, TILES, ring_to(side, stop - start), ring_recv.at[b])

    def other_on(b, side, k):
        for start, stop in OTHER_HOPS:
            if start == k and stop <= REACH[side] and CUTS[stop]:
                send(b, 0, CUTS[stop], ring_to(side, stop - start), ring_recv.at[b])

    def high_on(b, k):
        if CUTS[k] < TILES:
            for j in (1, 3, 2):
                send(b, CUTS[k], TILES, z_dev(j), z_cut_recv.at[b])

    for side in REACH:
        own_on(block, side, 0)
    for j in (1, 3, 2):
        send(block, 0, CUTS[0], z_dev(j), z_full_recv.at[zl])
    high_on(block, 0)
    to_mate(block, 0, TILES)

    new_master, new_one, new_two = adam(state[0], state[3], state[1], state[2], clip)
    master_out[...] = new_master
    one_out[...] = new_one
    two_out[...] = new_two

    def source(side, k):
        return rem(y - ahead * side * k + NY, NY) * NZL

    def hand_off():
        @pl.when(s > 0)
        def _():
            for m in range(NY):
                pltpu.make_async_remote_copy(
                    src_ref=part_b.at[m],
                    dst_ref=got_b.at[y],
                    send_sem=b_send,
                    recv_sem=b_recv,
                    device_id={"section": s - 1, "dp": (m * NZL + zl) * 2 + c},
                    device_id_type=MESH,
                ).start()

    for turn, (what, side, k, j) in enumerate(ORDER):
        if turn == HAND_OFF_TURN:
            hand_off()
        b = source(side, k) + z_other(j)
        if what == "own":
            drain(tiles(b, 0, TILES), ring_recv.at[b])
            own_on(b, side, k)
            high_on(b, k)
            to_mate(b, 0, TILES)
        elif what == "home":
            drain(tiles(b, 0, CUTS[0]), z_full_recv.at[z_other(j)])
            for out in REACH:
                other_on(b, out, 0)
            to_mate(b, 0, CUTS[0])
        elif what == "low":
            drain(tiles(b, 0, CUTS[k]), ring_recv.at[b])
            other_on(b, side, k)
            to_mate(b, 0, CUTS[k])
        else:
            drain(tiles(b, CUTS[k], TILES), z_cut_recv.at[b])
            to_mate(b, CUTS[k], TILES)

    @pl.when(s < 7)
    def _():
        drain(got_b, b_recv)
        rows = jnp.sum(got_b[...], axis=0)
        rows = [rows[u : u + 1, i * SLAB : (i + 1) * SLAB] for u in range(2) for i in range(4)]
        prev_out[...] = jnp.concatenate(rows, axis=0).astype(jnp.bfloat16)

    @pl.when(s == 7)
    def _():
        prev_out[...] = jnp.zeros_like(prev_out)

    for p, group in enumerate(groups):
        drain(norms[p].at[pl.ds(0, len(group))], norm_send.at[p])
    for i in range(4):
        drain(other.at[i], pair_send.at[i])
    drain(got_a.at[pl.ds(0, 7)], a_send)

    @pl.when(s > 0)
    def _():
        drain(got_b, b_send)

    for size, count in sorted(sent.items()):
        drain(w_out.at[0, pl.ds(0, count), :, pl.ds(0, size * 128)], gather_send.at[size])
    drain(w_out.at[1 - c], core_recv)
    drain(w_out.at[c], core_send)


def write_kernel(
    w, master, one, two, prev, prev_hbm, master_hbm, one_hbm, two_hbm, w_hbm, sem
):
    copies = []
    for h in range(2):
        rows = pl.ds(h * HALF, HALF)
        for b in range(32):
            copies.append(
                pltpu.make_async_copy(w.at[h, b], w_hbm.at[0, rows, pl.ds(b * WIDE, WIDE)], sem.at[b])
            )
    small = [
        pltpu.make_async_copy(prev, prev_hbm.at[0], sem.at[32 + 0]),
        pltpu.make_async_copy(master, master_hbm.at[0], sem.at[32 + 1]),
        pltpu.make_async_copy(one, one_hbm.at[0], sem.at[32 + 2]),
        pltpu.make_async_copy(two, two_hbm.at[0], sem.at[32 + 3]),
    ]
    for copy in small + copies:
        copy.start()
    for copy in small + copies:
        copy.wait()


def body(activations, out_grads, master, moment_one, moment_two):
    f32, bf16 = jnp.float32, jnp.bfloat16
    hbm = pl.BlockSpec(memory_space=pltpu.HBM)
    vmem = pl.BlockSpec(memory_space=pltpu.VMEM)
    dma = pltpu.SemaphoreType.DMA
    kept = pl.pallas_call(
        main_kernel,
        out_shape=(
            pltpu.VMEM((2, 32, HALF, WIDE), bf16),
            pltpu.VMEM((SLAB, COLS), f32),
            pltpu.VMEM((SLAB, COLS), f32),
            pltpu.VMEM((SLAB, COLS), f32),
            pltpu.VMEM((8, SLAB), bf16),
        ),
        in_specs=[hbm] * 5,
        out_specs=[vmem] * 5,
        scratch_shapes=[
            pltpu.VMEM((SLAB, 512), bf16),
            pltpu.VMEM((COLS, 512), bf16),
            pltpu.VMEM((4, SLAB, COLS), f32),
            pltpu.VMEM((4, HALF, COLS), f32),
            pltpu.VMEM((2 * NZ, 1, 128), f32),
            pltpu.VMEM((NX * NY, 1, 128), f32),
            pltpu.VMEM((512, SLAB), f32),
            pltpu.VMEM((8, 2, NY, 128), f32),
            pltpu.VMEM((8, 2, NY, 128), f32),
            pltpu.VMEM((NY, 2, 128), f32),
            pltpu.VMEM((NY, 2, 128), f32),
            dma((5,)), dma((2,)), dma((2,)), dma((4,)), dma((4,)),
            dma, dma, dma, dma,
            dma((TILES + 1,)), dma((32,)), dma, dma, dma((NZL,)), dma((32,)),
        ],
        compiler_params=pltpu.CompilerParams(
            collective_id=0, has_side_effects=True, vmem_limit_bytes=VMEM_GRANT
        ),
        name="update_and_gather",
    )(
        activations[0],
        jnp.swapaxes(out_grads, 1, 2)[0],
        master[0],
        moment_one[0],
        moment_two[0],
    )
    shapes = (
        jax.ShapeDtypeStruct((1, 8, SLAB), bf16),
        jax.ShapeDtypeStruct((1, SLAB, COLS), f32),
        jax.ShapeDtypeStruct((1, SLAB, COLS), f32),
        jax.ShapeDtypeStruct((1, SLAB, COLS), f32),
        jax.ShapeDtypeStruct((1, SLAB, FF), bf16),
    )
    return pl.pallas_call(
        write_kernel,
        out_shape=shapes,
        in_specs=[vmem] * 5,
        out_specs=[hbm] * 5,
        scratch_shapes=[dma((36,))],
        compiler_params=pltpu.CompilerParams(vmem_limit_bytes=8 << 20),
        name="write_out",
    )(*kept)


def solution(mesh):
    placed = (
        P("section", None, None),
        P("section", None, "dp"),
        P("section", None, "dp"),
        P("section", None, "dp"),
        P("section", None, "dp"),
    )
    return jax.shard_map(
        body,
        mesh=mesh,
        in_specs=placed,
        out_specs=(
            P("section", "dp", None),
            P("section", None, "dp"),
            P("section", None, "dp"),
            P("section", None, "dp"),
            P("section", None, None),
        ),
        check_vma=False,
    )
```

```python
import functools
import math

import jax
import jax.numpy as jnp
from jax import lax
from jax.experimental import pallas as pl
from jax.experimental.pallas import tpu as pltpu
from jax.sharding import PartitionSpec as P

FF = 53248
SLAB = 32
MESH = pl.DeviceIdType.MESH

NX, NY, NZ, NZL = 4, 8, 8, 4
COLS = FF // 64
WIDE = 2 * COLS
HALF = SLAB // 2
def hops(by, size):
    return min(by, size - by)


NEAR_STEPS = sorted(
    ((dz, dc) for dz in range(NZ) for dc in range(2) if dz or dc), key=lambda m: -hops(m[0], NZ)
)
FLAT_STEPS = sorted(
    ((dx, dy) for dx in range(NX) for dy in range(NY) if dx or dy),
    key=lambda m: -hops(m[0], NX) - hops(m[1], NY),
)
REACH = {1: 4, -1: 3}
OWN_HOPS = ((3, 4), (2, 3), (1, 2), (0, 1))
OTHER_HOPS = ((2, 4), (2, 3), (1, 2), (0, 1))
CUTS = (10, 10, 9, 9, 9)
TILES = WIDE // 128
HAND_OFF_TURN = 14
ORDER = (
    ("own", 1, 1, 0), ("own", -1, 1, 0), ("home", 1, 0, 3), ("home", 1, 0, 1), ("high", 1, 0, 3),
    ("high", 1, 0, 1), ("own", 1, 2, 0), ("home", 1, 0, 2), ("own", -1, 2, 0), ("high", 1, 1, 3),
    ("high", 1, 1, 1), ("high", 1, 0, 2), ("high", -1, 1, 3), ("low", 1, 1, 3), ("high", -1, 1, 1),
    ("low", -1, 1, 3), ("high", 1, 1, 2), ("low", 1, 1, 1), ("low", -1, 1, 1), ("high", -1, 1, 2),
    ("high", 1, 2, 3), ("high", 1, 2, 1), ("own", 1, 3, 0), ("low", -1, 1, 2), ("low", 1, 1, 2),
    ("high", -1, 2, 3), ("high", 1, 2, 2), ("high", -1, 2, 1), ("own", -1, 3, 0), ("low", 1, 2, 3),
    ("high", -1, 2, 2), ("low", -1, 2, 3), ("low", 1, 2, 1), ("low", -1, 2, 1), ("low", 1, 2, 2),
    ("low", -1, 2, 2), ("high", 1, 3, 3), ("high", 1, 3, 1), ("own", 1, 4, 0), ("high", 1, 3, 2),
    ("high", -1, 3, 3), ("high", -1, 3, 1), ("low", -1, 3, 3), ("high", -1, 3, 2), ("low", 1, 3, 3),
    ("low", -1, 3, 1), ("low", 1, 4, 3), ("low", -1, 3, 2), ("low", 1, 3, 1), ("low", 1, 4, 1),
    ("high", 1, 4, 3), ("low", 1, 3, 2), ("high", 1, 4, 1), ("low", 1, 4, 2), ("high", 1, 4, 2),
)
VMEM_GRANT = 63250000


def adam(master, grad, one, two, clip):
    scaled = clip * grad
    new_one = 0.9 * one + 0.1 * scaled
    new_two = 0.95 * two + 0.05 * scaled * scaled
    new_master = master - 0.05 * (new_one / (1.0 - 0.9**10)) / (
        jnp.sqrt(new_two / (1.0 - 0.95**10)) + 1e-08
    )
    return new_master, new_one, new_two


def main_kernel(
    acts_hbm, og_hbm, master_hbm, one_hbm, two_hbm,
    w_out, master_out, one_out, two_out, prev_out,
    acts, og, state, other, norms_near, norms_flat, turned, parts_a, got_a, part_b, got_b,
    load_sem, norm_send, norm_recv, pair_send, pair_recv,
    a_send, a_recv, b_send, b_recv,
    gather_send, ring_recv, core_send, core_recv, z_full_recv, z_cut_recv,
):
    s = lax.axis_index("section")
    d = lax.axis_index("dp")
    div, rem = lax.div, lax.rem
    norms = (norms_flat, norms_near)
    x, zh = div(s, 2), rem(s, 2)
    y, zl, c = div(d, 8), rem(div(d, 2), NZL), rem(d, 2)
    z = zh * NZL + zl

    def dev(x, y, z, c):
        return {"section": x * 2 + div(z, NZL), "dp": (y * NZL + rem(z, NZL)) * 2 + c}

    mate = dev(x, y, z, 1 - c)

    def ring8(a, by):
        return rem(a + by, 8)

    near = [dev(x, y, ring8(z, dz), rem(c + dc, 2)) for dz, dc in NEAR_STEPS]
    flat = [dev(rem(x + dx, NX), ring8(y, dy), z, c) for dx, dy in FLAT_STEPS]
    groups = (flat, near)
    places = (x * NY + y, z * 2 + c)
    place_a = zl * 2 + c
    group_a = [
        (rem(zl + dz, NZL) * 2 + rem(c + dc, 2), rem(zl + dz, NZL), rem(c + dc, 2))
        for dz in range(NZL)
        for dc in range(2)
        if dz or dc
    ]

    barrier = pltpu.get_barrier_semaphore()

    def greet(who):
        pl.semaphore_signal(barrier, inc=1, device_id=who, device_id_type=MESH)

    loads = [
        pltpu.make_async_copy(og_hbm, og, load_sem.at[0]),
        pltpu.make_async_copy(acts_hbm, acts, load_sem.at[1]),
        pltpu.make_async_copy(master_hbm, state.at[0], load_sem.at[2]),
        pltpu.make_async_copy(one_hbm, state.at[1], load_sem.at[3]),
        pltpu.make_async_copy(two_hbm, state.at[2], load_sem.at[4]),
    ]
    for load in loads:
        load.start()
    for group in groups:
        for who in group:
            greet(who)

    loads[1].wait()
    loads[0].wait()
    grad = lax.dot_general(
        acts[...], og[...], (((1,), (1,)), ((), ())), preferred_element_type=jnp.float32
    )
    state[3] = grad
    norms[0][places[0]] = jnp.broadcast_to(jnp.sum(grad * grad), (1, 128))
    pl.semaphore_wait(barrier, len(groups[0]) + len(groups[1]))

    def norm_start(p):
        for who in groups[p]:
            pltpu.make_async_remote_copy(
                src_ref=norms[p].at[places[p]],
                dst_ref=norms[p].at[places[p]],
                send_sem=norm_send.at[p],
                recv_sem=norm_recv.at[p],
                device_id=who,
                device_id_type=MESH,
            ).start()

    def drain(ref, sem):
        pltpu.make_async_copy(ref, ref, sem).wait()

    def norm_finish(p):
        drain(norms[p].at[pl.ds(0, len(groups[p]))], norm_recv.at[p])
        return jnp.sum(norms[p][...], axis=0)

    norm_start(0)

    for load in loads[2:]:
        load.wait()
    theirs = pl.ds(pl.multiple_of((1 - c) * HALF, HALF), HALF)
    mine = pl.ds(pl.multiple_of(c * HALF, HALF), HALF)
    for i in range(4):
        pltpu.make_async_remote_copy(
            src_ref=state.at[i, theirs],
            dst_ref=other.at[i],
            send_sem=pair_send.at[i],
            recv_sem=pair_recv.at[i],
            device_id=mate,
            device_id_type=MESH,
        ).start()

    weights = state[0].astype(jnp.bfloat16)
    partial = jnp.dot(weights, og[...], preferred_element_type=jnp.float32)
    turned[...] = partial.T
    for j in range(8):
        for u in range(2):
            rows = [pl.ds(j * 8 + u * 4 + i, NY, stride=64) for i in range(4)]
            parts_a[j, u] = jnp.concatenate([turned[r] for r in rows], axis=1)
    got_a[place_a] = parts_a[place_a]
    for m, to_zl, to_c in group_a:
        pltpu.make_async_remote_copy(
            src_ref=parts_a.at[m],
            dst_ref=got_a.at[place_a],
            send_sem=a_send,
            recv_sem=a_recv,
            device_id=dev(x, y, zh * NZL + to_zl, to_c),
            device_id_type=MESH,
        ).start()

    total = norm_finish(0)
    norms[1][places[1]] = total
    norm_start(1)

    drain(got_a.at[pl.ds(0, 7)], a_recv)
    for u in range(2):
        rows = jnp.sum(got_a[:, u], axis=0)
        for m in range(NY):
            part_b[m, u] = rows[m]

    for i in range(4):
        drain(other.at[i], pair_recv.at[i])

    total = norm_finish(1)
    limit = math.sqrt(8 * FF * SLAB)
    clip = jnp.minimum(1.0, limit / jnp.sqrt(total + 1e-06))[:, :1]

    own_w, _, _ = adam(state[0, mine], state[3, mine], state[1, mine], state[2, mine], clip)
    mate_w, _, _ = adam(other[0], other[3], other[1], other[2], clip)
    first = jnp.where(c == 0, own_w, mate_w)
    second = jnp.where(c == 0, mate_w, own_w)
    block = y * NZL + zl
    whole = jnp.concatenate([first, second], axis=1).astype(jnp.bfloat16)
    w_out[c, block] = whole

    ahead = 1 - 2 * c

    def ring_to(side, hops):
        return dev(x, rem(y + ahead * side * hops + NY, NY), z, c)

    def tiles(b, start, stop):
        return w_out.at[c, b, :, pl.ds(start * 128, (stop - start) * 128)]

    sent = {}

    def send(b, start, stop, to, recv_sem):
        size = stop - start
        sent[size] = sent.get(size, 0) + 1
        ref = tiles(b, start, stop)
        pltpu.make_async_remote_copy(
            src_ref=ref, dst_ref=ref, send_sem=gather_send.at[size], recv_sem=recv_sem,
            device_id=to, device_id_type=MESH,
        ).start()

    def to_mate(b, start, stop):
        ref = tiles(b, start, stop)
        pltpu.make_async_remote_copy(
            src_ref=ref, dst_ref=ref, send_sem=core_send, recv_sem=core_recv,
            device_id=mate, device_id_type=MESH,
        ).start()

    def z_other(j):
        return rem(zl + j, NZL)

    def z_dev(j):
        return dev(x, y, zh * NZL + z_other(j), c)

    def own_on(b, side, k):
        for start, stop in OWN_HOPS:
            if start == k and stop <= REACH[side]:
                send(b, 0, TILES, ring_to(side, stop - start), ring_recv.at[b])

    def other_on(b, side, k):
        for start, stop in OTHER_HOPS:
            if start == k and stop <= REACH[side] and CUTS[stop]:
                send(b, 0, CUTS[stop], ring_to(side, stop - start), ring_recv.at[b])

    def high_on(b, k):
        if CUTS[k] < TILES:
            for j in (1, 3, 2):
                send(b, CUTS[k], TILES, z_dev(j), z_cut_recv.at[b])

    for side in REACH:
        own_on(block, side, 0)
    for j in (1, 3, 2):
        send(block, 0, CUTS[0], z_dev(j), z_full_recv.at[zl])
    high_on(block, 0)
    to_mate(block, 0, TILES)

    def source(side, k):
        return rem(y - ahead * side * k + NY, NY) * NZL

    def hand_off():
        @pl.when(s > 0)
        def _():
            for m in range(NY):
                pltpu.make_async_remote_copy(
                    src_ref=part_b.at[m],
                    dst_ref=got_b.at[y],
                    send_sem=b_send,
                    recv_sem=b_recv,
                    device_id={"section": s - 1, "dp": (m * NZL + zl) * 2 + c},
                    device_id_type=MESH,
                ).start()

    for turn, (what, side, k, j) in enumerate(ORDER):
        if turn == HAND_OFF_TURN:
            hand_off()
        b = source(side, k) + z_other(j)
        if what == "own":
            drain(tiles(b, 0, TILES), ring_recv.at[b])
            own_on(b, side, k)
            high_on(b, k)
            to_mate(b, 0, TILES)
        elif what == "home":
            drain(tiles(b, 0, CUTS[0]), z_full_recv.at[z_other(j)])
            for out in REACH:
                other_on(b, out, 0)
            to_mate(b, 0, CUTS[0])
        elif what == "low":
            drain(tiles(b, 0, CUTS[k]), ring_recv.at[b])
            other_on(b, side, k)
            to_mate(b, 0, CUTS[k])
        else:
            drain(tiles(b, CUTS[k], TILES), z_cut_recv.at[b])
            to_mate(b, CUTS[k], TILES)

    new_master, new_one, new_two = adam(state[0], state[3], state[1], state[2], clip)
    master_out[...] = new_master
    one_out[...] = new_one
    two_out[...] = new_two

    @pl.when(s < 7)
    def _():
        drain(got_b, b_recv)
        rows = jnp.sum(got_b[...], axis=0)
        rows = [rows[u : u + 1, i * SLAB : (i + 1) * SLAB] for u in range(2) for i in range(4)]
        prev_out[...] = jnp.concatenate(rows, axis=0).astype(jnp.bfloat16)

    @pl.when(s == 7)
    def _():
        prev_out[...] = jnp.zeros_like(prev_out)

    for p, group in enumerate(groups):
        drain(norms[p].at[pl.ds(0, len(group))], norm_send.at[p])
    for i in range(4):
        drain(other.at[i], pair_send.at[i])
    drain(got_a.at[pl.ds(0, 7)], a_send)

    @pl.when(s > 0)
    def _():
        drain(got_b, b_send)

    for size, count in sorted(sent.items()):
        drain(w_out.at[0, pl.ds(0, count), :, pl.ds(0, size * 128)], gather_send.at[size])
    drain(w_out.at[1 - c], core_recv)
    drain(w_out.at[c], core_send)


def write_kernel(
    w, master, one, two, prev, prev_hbm, master_hbm, one_hbm, two_hbm, w_hbm, sem
):
    copies = []
    for h in range(2):
        rows = pl.ds(h * HALF, HALF)
        for b in range(32):
            copies.append(
                pltpu.make_async_copy(w.at[h, b], w_hbm.at[0, rows, pl.ds(b * WIDE, WIDE)], sem.at[b])
            )
    small = [
        pltpu.make_async_copy(prev, prev_hbm.at[0], sem.at[32 + 0]),
        pltpu.make_async_copy(master, master_hbm.at[0], sem.at[32 + 1]),
        pltpu.make_async_copy(one, one_hbm.at[0], sem.at[32 + 2]),
        pltpu.make_async_copy(two, two_hbm.at[0], sem.at[32 + 3]),
    ]
    for copy in small + copies:
        copy.start()
    for copy in small + copies:
        copy.wait()


def body(activations, out_grads, master, moment_one, moment_two):
    f32, bf16 = jnp.float32, jnp.bfloat16
    hbm = pl.BlockSpec(memory_space=pltpu.HBM)
    vmem = pl.BlockSpec(memory_space=pltpu.VMEM)
    dma = pltpu.SemaphoreType.DMA
    kept = pl.pallas_call(
        main_kernel,
        out_shape=(
            pltpu.VMEM((2, 32, HALF, WIDE), bf16),
            pltpu.VMEM((SLAB, COLS), f32),
            pltpu.VMEM((SLAB, COLS), f32),
            pltpu.VMEM((SLAB, COLS), f32),
            pltpu.VMEM((8, SLAB), bf16),
        ),
        in_specs=[hbm] * 5,
        out_specs=[vmem] * 5,
        scratch_shapes=[
            pltpu.VMEM((SLAB, 512), bf16),
            pltpu.VMEM((COLS, 512), bf16),
            pltpu.VMEM((4, SLAB, COLS), f32),
            pltpu.VMEM((4, HALF, COLS), f32),
            pltpu.VMEM((2 * NZ, 1, 128), f32),
            pltpu.VMEM((NX * NY, 1, 128), f32),
            pltpu.VMEM((512, SLAB), f32),
            pltpu.VMEM((8, 2, NY, 128), f32),
            pltpu.VMEM((8, 2, NY, 128), f32),
            pltpu.VMEM((NY, 2, 128), f32),
            pltpu.VMEM((NY, 2, 128), f32),
            dma((5,)), dma((2,)), dma((2,)), dma((4,)), dma((4,)),
            dma, dma, dma, dma,
            dma((TILES + 1,)), dma((32,)), dma, dma, dma((NZL,)), dma((32,)),
        ],
        compiler_params=pltpu.CompilerParams(
            collective_id=0, has_side_effects=True, vmem_limit_bytes=VMEM_GRANT
        ),
        name="update_and_gather",
    )(
        activations[0],
        jnp.swapaxes(out_grads, 1, 2)[0],
        master[0],
        moment_one[0],
        moment_two[0],
    )
    shapes = (
        jax.ShapeDtypeStruct((1, 8, SLAB), bf16),
        jax.ShapeDtypeStruct((1, SLAB, COLS), f32),
        jax.ShapeDtypeStruct((1, SLAB, COLS), f32),
        jax.ShapeDtypeStruct((1, SLAB, COLS), f32),
        jax.ShapeDtypeStruct((1, SLAB, FF), bf16),
    )
    return pl.pallas_call(
        write_kernel,
        out_shape=shapes,
        in_specs=[vmem] * 5,
        out_specs=[hbm] * 5,
        scratch_shapes=[dma((36,))],
        compiler_params=pltpu.CompilerParams(vmem_limit_bytes=8 << 20),
        name="write_out",
    )(*kept)


def solution(mesh):
    placed = (
        P("section", None, None),
        P("section", None, "dp"),
        P("section", None, "dp"),
        P("section", None, "dp"),
        P("section", None, "dp"),
    )
    return jax.shard_map(
        body,
        mesh=mesh,
        in_specs=placed,
        out_specs=(
            P("section", "dp", None),
            P("section", None, "dp"),
            P("section", None, "dp"),
            P("section", None, "dp"),
            P("section", None, None),
        ),
        check_vma=False,
    )
```
